32 devices in a mesh: row: 8 (over y, x, core), col: 4 (over z).
Axes of the slice: x: 2, y: 2, z: 4, core: 2. Of those that a mesh axis runs over, the one named last changes fastest.
Arguments:
- act_tiles: bfloat16 [3072, 2048], P('row', 'col'), may hold values from -6 to 6
- up_tiles: bfloat16 [2048, 3584], P('row', 'col'), may hold values from -0.125 to 0.125
Outputs:
- hidden_act: bfloat16 [3072, 3584], P('row', 'col')
The draws below stay inside these ranges and needn't reach their ends.
All inputs are finite; a program needn't handle non-finite values.
Results may differ from the reference program's by a relative error of at most 0.001.
Values may be sent and summed in bfloat16 or wider, within the bound.
A program may use at most 64 MiB of HBM per device.

```python
import jax
import jax.numpy as jnp
from jax import lax

TOK_DEV = 384
KB = 256
HID_DEV = 896
D = 2048
TOKENS = 3072
FF = 3584
N_ROW = 8
N_COL = 4


def shard_levels(own_key, shape, split, smallest, top_value):
    factor_of = 1.0
    for axis_at, parts in split:
        draws = jax.random.uniform(jax.random.fold_in(jax.random.fold_in(own_key, 6), axis_at), (parts,), jnp.float32, smallest / len(split), top_value / len(split))
        factor_of = factor_of * jnp.repeat(jnp.exp(draws), shape[axis_at] // parts).reshape((-1,) + (1,) * (len(shape) - 1 - axis_at))
    return factor_of


def bell_draw(key, dims, deviation, most, cuts=(), held_as=jnp.bfloat16):
    drawn = deviation * jax.random.normal(key, dims, jnp.float32)
    if cuts:
        drawn = drawn * shard_levels(key, dims, cuts, -0.22, 0.18)
    return jnp.clip(drawn, -most, most).astype(held_as)


def setup_inputs(seed: int = 0) -> dict:
    streams_of = jax.random.split(jax.random.key(seed), 3)
    act_tiles = bell_draw(streams_of[0], (TOKENS, D), 1.0, 6.0, ((0, 8), (1, 4)))
    up_tiles = bell_draw(streams_of[1], (D, FF), D ** -0.5, 0.125, ((0, 8), (1, 4)))
    return dict(act_tiles=act_tiles, up_tiles=up_tiles)


def reference(act_tiles, up_tiles):
    block_ids = jnp.arange(N_ROW, dtype=jnp.int32)
    act_blocks = act_tiles.reshape(N_ROW, TOK_DEV, N_ROW, KB)

    def unskew_row(blocks, row_index):
        return jnp.take(blocks, (block_ids - row_index) % N_ROW, axis=1)

    features = jax.vmap(unskew_row)(act_blocks, block_ids).reshape(N_ROW * TOK_DEV, N_ROW * KB).astype(jnp.float32)
    up_blocks = up_tiles.reshape(N_ROW, KB, N_COL, HID_DEV)

    def column_block(col_index):
        column = lax.dynamic_index_in_dim(up_blocks, col_index, 2, keepdims=False)
        weights = jnp.take(column, (block_ids - 2 * col_index) % N_ROW, axis=0).reshape(N_ROW * KB, HID_DEV).astype(jnp.float32)
        pre = jnp.dot(features, weights, preferred_element_type=jnp.float32, precision=lax.Precision.HIGHEST)
        return jax.nn.silu(pre).astype(jnp.bfloat16)

    result = lax.map(column_block, jnp.arange(N_COL, dtype=jnp.int32))
    return jnp.transpose(result, (1, 0, 2)).reshape(N_ROW * TOK_DEV, N_COL * HID_DEV)
```

```python
import functools

import jax
import jax.numpy as jnp
from jax import lax
from jax.experimental import pallas as pl
from jax.experimental.pallas import tpu as pltpu
from jax.sharding import PartitionSpec as P

MESH = pl.DeviceIdType.MESH


def pieces_of(rows, wanted, multiple):
    return max(n for n in range(1, wanted + 1) if rows % (n * multiple) == 0)


def pieces_halved(rows, wanted, multiple):
    pieces = []
    while len(pieces) < wanted - 1 and rows % (2 * multiple) == 0:
        rows //= 2
        pieces.append(rows)
    return pieces + [rows]


def kernel(grid, counts, a_hbm, w_hbm, out, acts, weights, total, send_a, recv_a, send_w, recv_w, share_w, local_sem, go):
    n_y, n_x, n_col = grid
    n_a, n_w = counts
    n_row = 2 * n_y * n_x
    tokens, width = acts.shape[1:]
    depth, hidden = weights.shape[1:]
    per = width // depth
    row_w = depth // n_w
    starts_a = [sum(n_a[:k]) for k in range(len(n_a))]
    sizes_a, n_a = n_a, len(n_a)

    r, c = lax.axis_index("row"), lax.axis_index("col")
    core = lax.rem(r, 2)
    x = lax.rem(r // 2, n_x)
    y = r // (2 * n_x)
    last = n_col - 1

    def row_of(dy, dx, other_core=False):
        which = 1 - core if other_core else core
        return (lax.rem(y + dy, n_y) * n_x + lax.rem(x + dx, n_x)) * 2 + which

    pair = row_of(0, 0, True)
    peers_x = [(0, dx) for dx in range(1, n_x)]
    peers_y = [(dy, 0) for dy in range(1, n_y)]
    diagonal = [(dy, dx) for dy in range(1, n_y) for dx in range(1, n_x)]
    near = [row_of(*p) for p in peers_x + peers_y]
    far = [row_of(*p) for p in diagonal]
    row_peers = near + [pair]

    def weight_at(source, owner, k):
        rel = lax.rem(source - owner + n_row, n_row)
        return weights.at[rel, pl.ds(k * row_w, row_w)]

    def weight_copy(source, to, recv, k, own=False):
        return pltpu.make_async_remote_copy(
            src_ref=w_hbm.at[pl.ds(k * row_w, row_w)] if own else weight_at(source, r, k),
            dst_ref=weight_at(source, to, k),
            send_sem=send_w,
            recv_sem=recv,
            device_id=(to, c),
            device_id_type=MESH,
        )

    def act_copy(source, side, k, own=False):
        rows = pl.ds(starts_a[k], sizes_a[k])
        return pltpu.make_async_remote_copy(
            src_ref=a_hbm.at[rows] if own else acts.at[source, rows],
            dst_ref=acts.at[source, rows],
            send_sem=send_a.at[side],
            recv_sem=recv_a.at[source, k],
            device_id=(r, c + 2 * side - 1),
            device_id_type=MESH,
        )

    def filled(ref, sem):
        pltpu.make_async_copy(ref, ref, sem).wait()

    barrier = pltpu.get_barrier_semaphore()

    def greet(to):
        pl.semaphore_signal(barrier, inc=1, device_id=to, device_id_type=MESH)

    def tell(to):
        pl.semaphore_signal(go, inc=1, device_id=to, device_id_type=MESH)

    early = c == 1

    @pl.when(jnp.logical_and(c < last, c != 0))
    def _():
        greet((r, c + 1))

    @pl.when(jnp.logical_and(c > 0, c != 2))
    def _():
        greet((r, c - 1))

    @pl.when(jnp.logical_and(c == 0, c < last))
    def _():
        greet((r, c + 1))

    @pl.when(jnp.logical_not(early))
    def _():
        for to in row_peers:
            greet((to, c))

    own_a = pltpu.make_async_copy(a_hbm, acts.at[c], local_sem.at[0])
    own_w = pltpu.make_async_copy(w_hbm, weights.at[0], local_sem.at[1])
    own_a.start()
    own_w.start()

    def own_acts(side):
        for k in range(n_a):
            act_copy(c, side, k, True).start()

    @pl.when(early)
    def _():
        pl.semaphore_wait(barrier, 1)
        own_acts(0)
        pl.semaphore_wait(go, 2 if n_col > 2 else 1)

    @pl.when(jnp.logical_not(early))
    def _():
        beside = jnp.where(c > 0, 1, 0) + jnp.where(c < last, 1, 0)
        pl.semaphore_wait(barrier, len(row_peers) + beside)

        @pl.when(c > 0)
        def _():
            own_acts(0)

        @pl.when(c == 2)
        def _():
            tell((r, c - 1))

    @pl.when(jnp.logical_and(c == 0, c < last))
    def _():
        for to in row_peers:
            tell((to, c))

    @pl.when(c < last)
    def _():
        own_acts(1)

    for k in range(n_w):
        for to in near:
            weight_copy(r, to, recv_w.at[0, k], k, True).start()
        weight_copy(r, pair, share_w, k, True).start()

    @pl.when(jnp.logical_and(c == 0, c < last))
    def _():
        pl.semaphore_wait(go, len(row_peers))
        tell((r, c + 1))

    def first_weights(k):
        filled(weights.at[pl.ds(0, len(near)), pl.ds(0, row_w)], recv_w.at[0, k])
        for dy, dx in diagonal:
            @pl.when(core == 0)
            def _():
                weight_copy(row_of(dy, 0), row_of(0, dx), recv_w.at[1, k], k).start()

            @pl.when(core == 1)
            def _():
                weight_copy(row_of(0, dx), row_of(dy, 0), recv_w.at[1, k], k).start()
        for source in near:
            weight_copy(source, pair, share_w, k).start()

    def far_weights(k):
        filled(weights.at[pl.ds(0, len(far)), pl.ds(0, row_w)], recv_w.at[1, k])
        for source in far:
            weight_copy(source, pair, share_w, k).start()

    short = jnp.minimum(c, last - c)
    toward = jnp.where(last - c >= c, 1, -1)

    def source_at(t):
        near_step = t // 2 + 1
        near_sign = toward * (1 - 2 * lax.rem(t, 2))
        return jnp.where(t < 2 * short, c + near_sign * near_step, c + toward * (t - short + 1))

    inner = jnp.logical_and(c > 0, c < last)

    def pass_acts(t, k):
        source = source_at(t)
        act_copy(source, 0, k).wait_recv()

        @pl.when(source < c)
        def _():
            act_copy(source, 1, k).start()

        @pl.when(source > c)
        def _():
            act_copy(source, 0, k).start()

    events = []
    a_time, w_time = tokens // n_a * width, row_w * hidden
    for t in range(last):
        for k in range(n_a):
            events.append(((t // 2 * n_a + k + 1) * a_time, "a", t, k))
    for k in range(n_w):
        events.append(((k + 1) * w_time * (n_x + n_y - 2) / 2, "near", 0, k))
        events.append(((k + 2) * w_time * (n_x + n_y - 2) / 2 + w_time, "far", 0, k))
    for _, kind, t, k in sorted(events):
        if kind == "a":
            pl.when(inner)(functools.partial(pass_acts, t, k))
        elif kind == "near":
            first_weights(k)
        elif diagonal:
            far_weights(k)
    filled(weights.at[pl.ds(0, n_row // 2)], share_w)
    own_w.wait()
    own_a.wait()

    def product(source, rows):
        at = lax.rem(source - c + n_col, n_col)
        held = weights[pl.ds(at * per, per)].reshape(width, hidden)
        return jnp.dot(acts[source, rows, :], held, preferred_element_type=jnp.float32)

    every = pl.ds(0, tokens)
    total[...] = product(c, every)

    @pl.loop(0, last - 1)
    def _(t):
        source = source_at(t)

        @pl.when(jnp.logical_not(inner))
        def _():
            for k in range(n_a):
                act_copy(source, 0, k).wait_recv()

        total[...] += product(source, every)

    final = source_at(last - 1)

    for k in range(n_a):
        rows = pl.ds(starts_a[k], sizes_a[k])

        pl.when(jnp.logical_not(inner))(act_copy(final, 0, k).wait_recv)

        pre = total[rows, :] + product(final, rows)
        out[rows, :] = (pre / (1.0 + jnp.exp(-pre))).astype(out.dtype)

    for n in range(1, n_col):
        pl.when(jnp.logical_and(c < last, c + 1 == n))(functools.partial(filled, acts.at[pl.ds(0, n)], send_a.at[1]))
        pl.when(jnp.logical_and(c > 0, n_col - c == n))(functools.partial(filled, acts.at[pl.ds(0, n)], send_a.at[0]))
    filled(weights.at[pl.ds(0, n_row - 1)], send_w)


def body(n_row, n_col, act_tiles, up_tiles):
    tokens, width = act_tiles.shape
    depth, hidden = up_tiles.shape
    chips = n_row // 2
    n_x = max(n for n in range(1, chips + 1) if chips % n == 0 and n * n <= chips)
    n_y = chips // n_x
    cuts, n_w = pieces_halved(tokens, 3, 16), pieces_of(depth, 2, 16)
    n_a = len(cuts)
    return pl.pallas_call(
        functools.partial(kernel, (n_y, n_x, n_col), (cuts, n_w)),
        out_shape=pltpu.VMEM((tokens, hidden), jnp.bfloat16),
        in_specs=[pl.BlockSpec(memory_space=pltpu.HBM)] * 2,
        out_specs=pl.BlockSpec(memory_space=pltpu.VMEM),
        scratch_shapes=[
            pltpu.VMEM((n_col, tokens, width), jnp.bfloat16),
            pltpu.VMEM((n_row, depth, hidden), jnp.bfloat16),
            pltpu.VMEM((tokens, hidden), jnp.float32),
            pltpu.SemaphoreType.DMA((2,)),
            pltpu.SemaphoreType.DMA((n_col, n_a)),
            pltpu.SemaphoreType.DMA,
            pltpu.SemaphoreType.DMA((2, n_w)),
            pltpu.SemaphoreType.DMA,
            pltpu.SemaphoreType.DMA((2,)),
            pltpu.SemaphoreType.REGULAR,
        ],
        compiler_params=pltpu.CompilerParams(collective_id=0, has_side_effects=True, vmem_limit_bytes=60000000),
        cost_estimate=pl.CostEstimate(
            flops=2 * tokens * width * n_col * hidden,
            bytes_accessed=2 * (act_tiles.size + up_tiles.size + tokens * hidden),
            transcendentals=tokens * hidden,
        ),
        name="gather_up_silu",
    )(act_tiles, up_tiles)


def solution(mesh):
    return jax.shard_map(
        functools.partial(body, mesh.shape["row"], mesh.shape["col"]),
        mesh=mesh,
        in_specs=(P("row", "col"), P("row", "col")),
        out_specs=P("row", "col"),
        check_vma=False,
    )
```

```python
import functools

import jax
import jax.numpy as jnp
from jax import lax
from jax.experimental import pallas as pl
from jax.experimental.pallas import tpu as pltpu
from jax.sharding import PartitionSpec as P

MESH = pl.DeviceIdType.MESH


def pieces_of(rows, wanted, multiple):
    return max(n for n in range(1, wanted + 1) if rows % (n * multiple) == 0)


def pieces_uneven(rows, shares, multiple):
    unit = rows // sum(shares)
    return [n * unit for n in shares] if unit * sum(shares) == rows and unit % multiple == 0 else [rows]


def kernel(grid, counts, a_hbm, w_hbm, out, acts, weights, total, send_a, recv_a, send_w, recv_w, share_w, local_sem, go, held, send_h, recv_h):
    n_y, n_x, n_col = grid
    n_a, n_w = counts
    n_row = 2 * n_y * n_x
    tokens, width = acts.shape[1:]
    depth, hidden = weights.shape[1:]
    per = width // depth
    row_w = depth // n_w
    starts_a = [sum(n_a[:k]) for k in range(len(n_a))]
    sizes_a, n_a = n_a, len(n_a)

    r, c = lax.axis_index("row"), lax.axis_index("col")
    core = lax.rem(r, 2)
    x = lax.rem(r // 2, n_x)
    y = r // (2 * n_x)
    last = n_col - 1

    def row_of(dy, dx, other_core=False):
        which = 1 - core if other_core else core
        return (lax.rem(y + dy, n_y) * n_x + lax.rem(x + dx, n_x)) * 2 + which

    pair = row_of(0, 0, True)
    peers_x = [(0, dx) for dx in range(1, n_x)]
    peers_y = [(dy, 0) for dy in range(1, n_y)]
    diagonal = [(dy, dx) for dy in range(1, n_y) for dx in range(1, n_x)]
    near = [row_of(*p) for p in peers_x + peers_y]
    far = [row_of(*p) for p in diagonal]
    row_peers = near + [pair]

    helpers = []
    if n_a > 2 and n_col > 1:
        helpers += [(3, n_a - 2)] if n_x > 1 else []
        helpers += [(2 * n_x + 1, n_a - 1)] if n_y > 1 else []

    def weight_at(source, owner, k):
        rel = lax.rem(source - owner + n_row, n_row)
        return weights.at[rel, pl.ds(k * row_w, row_w)]

    def weight_copy(source, to, recv, k, own=False):
        return pltpu.make_async_remote_copy(
            src_ref=w_hbm.at[pl.ds(k * row_w, row_w)] if own else weight_at(source, r, k),
            dst_ref=weight_at(source, to, k),
            send_sem=send_w,
            recv_sem=recv,
            device_id=(to, c),
            device_id_type=MESH,
        )

    def act_copy(source, side, k, own=False, arrives=False):
        to = c if arrives else c + 2 * side - 1
        rows = pl.ds(starts_a[k], sizes_a[k])
        return pltpu.make_async_remote_copy(
            src_ref=a_hbm.at[rows] if own else acts.at[source, rows],
            dst_ref=acts.at[source, rows],
            send_sem=send_a.at[side],
            recv_sem=recv_a.at[lax.rem(source - to + n_col, n_col) - 1, k],
            device_id=(r, to),
            device_id_type=MESH,
        )

    def held_copy(src, dst, to, send, recv):
        return pltpu.make_async_remote_copy(
            src_ref=src, dst_ref=dst, send_sem=send, recv_sem=recv, device_id=to, device_id_type=MESH
        )

    def wait_acts(source, k):
        act_copy(source, 0, k, arrives=True).wait_recv()

    def filled(ref, sem):
        pltpu.make_async_copy(ref, ref, sem).wait()

    barrier = pltpu.get_barrier_semaphore()

    def greet(to):
        pl.semaphore_signal(barrier, inc=1, device_id=to, device_id_type=MESH)

    def tell(to):
        pl.semaphore_signal(go, inc=1, device_id=to, device_id_type=MESH)

    early = c == 1

    @pl.when(jnp.logical_and(c < last, c != 0))
    def _():
        greet((r, c + 1))

    @pl.when(jnp.logical_and(c > 0, c != 2))
    def _():
        greet((r, c - 1))

    @pl.when(jnp.logical_and(c == 0, c < last))
    def _():
        greet((r, c + 1))

    @pl.when(jnp.logical_not(early))
    def _():
        for to in row_peers:
            greet((to, c))

    for helper, _ in helpers:
        @pl.when(jnp.logical_and(c == 0, r == 0))
        def _():
            greet((helper, 0))

        @pl.when(jnp.logical_and(c == 0, r == helper))
        def _():
            greet((0, 0))

    helped = jnp.where(r == 0, len(helpers), sum((jnp.where(r == helper, 1, 0) for helper, _ in helpers), 0))
    helped = jnp.where(c == 0, helped, 0)

    own_a = pltpu.make_async_copy(a_hbm, acts.at[c], local_sem.at[0])
    own_w = pltpu.make_async_copy(w_hbm, weights.at[0], local_sem.at[1])
    own_a.start()
    own_w.start()

    def own_acts(side):
        for k in range(n_a):
            act_copy(c, side, k, True).start()

    @pl.when(early)
    def _():
        pl.semaphore_wait(barrier, 1)
        for k in range(n_a):
            if k in [taken for _, taken in helpers]:
                pl.when(r != 0)(act_copy(c, 0, k, True).start)
            else:
                act_copy(c, 0, k, True).start()
        pl.semaphore_wait(go, 2 if n_col > 2 else 1)

        @pl.when(r == 0)
        def _():
            for helper, k in helpers:
                held_copy(a_hbm.at[pl.ds(starts_a[k], sizes_a[k])], held, (helper, 1), send_a.at[0], recv_h).start()

    @pl.when(jnp.logical_not(early))
    def _():
        beside = jnp.where(c > 0, 1, 0) + jnp.where(c < last, 1, 0)
        pl.semaphore_wait(barrier, len(row_peers) + beside + helped)

        @pl.when(c > 0)
        def _():
            own_acts(0)

        @pl.when(c == 2)
        def _():
            tell((r, c - 1))

    @pl.when(jnp.logical_and(c == 0, c < last))
    def _():
        for to in row_peers:
            tell((to, c))
        for helper, _ in helpers:
            pl.when(r == helper)(functools.partial(tell, (0, c)))

    @pl.when(c < last)
    def _():
        own_acts(1)

    for k in range(n_w):
        for to in near:
            weight_copy(r, to, recv_w.at[0, k], k, True).start()
        weight_copy(r, pair, share_w, k, True).start()

    @pl.when(jnp.logical_and(c == 0, c < last))
    def _():
        pl.semaphore_wait(go, len(row_peers) + jnp.where(r == 0, len(helpers), 0))
        tell((r, c + 1))

    def first_weights(k):
        filled(weights.at[pl.ds(0, len(near)), pl.ds(0, row_w)], recv_w.at[0, k])
        for dy, dx in diagonal:
            @pl.when(core == 0)
            def _():
                weight_copy(row_of(dy, 0), row_of(0, dx), recv_w.at[1, k], k).start()

            @pl.when(core == 1)
            def _():
                weight_copy(row_of(0, dx), row_of(dy, 0), recv_w.at[1, k], k).start()
        for source in near:
            weight_copy(source, pair, share_w, k).start()

    def far_weights(k):
        filled(weights.at[pl.ds(0, len(far)), pl.ds(0, row_w)], recv_w.at[1, k])
        for source in far:
            weight_copy(source, pair, share_w, k).start()

    short = jnp.minimum(c, last - c)
    toward = jnp.where(last - c >= c, 1, -1)

    def source_at(t):
        near_step = t // 2 + 1
        near_sign = toward * (1 - 2 * lax.rem(t, 2))
        return jnp.where(t < 2 * short, c + near_sign * near_step, c + toward * (t - short + 1))

    inner = jnp.logical_and(c > 0, c < last)

    def pass_acts(t, k):
        source = source_at(t)
        wait_acts(source, k)

        @pl.when(source < c)
        def _():
            act_copy(source, 1, k).start()

        @pl.when(source > c)
        def _():
            act_copy(source, 0, k).start()

    def help_out():
        for helper, k in helpers:
            @pl.when(jnp.logical_and(c == 1, r == helper))
            def _():
                filled(held, recv_h)
                held_copy(held, held, (r, 0), send_h, recv_h).start()

    def help_in():
        for helper, k in helpers:
            @pl.when(jnp.logical_and(c == 0, r == helper))
            def _():
                filled(held, recv_h)
                there = acts.at[1, pl.ds(starts_a[k], sizes_a[k])]
                held_copy(held, there, (0, 0), send_h, recv_a.at[0, k]).start()

    events = [(0.4 * tokens * width, "out", 0, 0), (1.1 * tokens * width, "in", 0, 0)]
    w_time, w_lag = row_w * hidden, tokens * width / 10
    for t in range(last):
        for k in range(n_a):
            events.append(((t // 2 * tokens + starts_a[k] + sizes_a[k]) * width, "a", t, k))
    for k in range(n_w):
        events.append(((k + 1) * w_time * (n_x + n_y - 2) / 2 + w_lag, "near", 0, k))
        events.append(((k + 2) * w_time * (n_x + n_y - 2) / 2 + w_time + w_lag, "far", 0, k))
    for _, kind, t, k in sorted(events):
        if kind == "a":
            pl.when(inner)(functools.partial(pass_acts, t, k))
        elif kind == "out":
            help_out()
        elif kind == "in":
            help_in()
        elif kind == "near":
            first_weights(k)
        elif diagonal:
            far_weights(k)
    filled(weights.at[pl.ds(0, n_row // 2)], share_w)
    own_w.wait()
    own_a.wait()

    def product(source, rows):
        at = lax.rem(source - c + n_col, n_col)
        held = weights[pl.ds(at * per, per)].reshape(width, hidden)
        return jnp.dot(acts[source, rows, :], held, preferred_element_type=jnp.float32)

    every = pl.ds(0, tokens)
    total[...] = product(c, every)

    @pl.loop(0, last - 1)
    def _(t):
        source = source_at(t)

        @pl.when(jnp.logical_not(inner))
        def _():
            for k in range(n_a):
                wait_acts(source, k)

        total[...] += product(source, every)

    final = source_at(last - 1)

    for k in range(n_a):
        rows = pl.ds(starts_a[k], sizes_a[k])

        pl.when(jnp.logical_not(inner))(functools.partial(wait_acts, final, k))

        pre = total[rows, :] + product(final, rows)
        out[rows, :] = (pre / (1.0 + jnp.exp(-pre))).astype(out.dtype)

    for n in range(1, n_col):
        pl.when(jnp.logical_and(c < last, c + 1 == n))(functools.partial(filled, acts.at[pl.ds(0, n)], send_a.at[1]))
        pl.when(jnp.logical_and(c > 0, n_col - c == n))(functools.partial(filled, acts.at[pl.ds(0, n)], send_a.at[0]))
    for helper, _ in helpers:
        pl.when(jnp.logical_and(c < 2, r == helper))(functools.partial(filled, held, send_h))
    filled(weights.at[pl.ds(0, n_row - 1)], send_w)


def body(n_row, n_col, act_tiles, up_tiles):
    tokens, width = act_tiles.shape
    depth, hidden = up_tiles.shape
    chips = n_row // 2
    n_x = max(n for n in range(1, chips + 1) if chips % n == 0 and n * n <= chips)
    n_y = chips // n_x
    cuts, n_w = pieces_uneven(tokens, (2, 4, 1, 1), 16), pieces_of(depth, 2, 16)
    n_a = len(cuts)
    return pl.pallas_call(
        functools.partial(kernel, (n_y, n_x, n_col), (cuts, n_w)),
        out_shape=pltpu.VMEM((tokens, hidden), jnp.bfloat16),
        in_specs=[pl.BlockSpec(memory_space=pltpu.HBM)] * 2,
        out_specs=pl.BlockSpec(memory_space=pltpu.VMEM),
        scratch_shapes=[
            pltpu.VMEM((n_col, tokens, width), jnp.bfloat16),
            pltpu.VMEM((n_row, depth, hidden), jnp.bfloat16),
            pltpu.VMEM((tokens, hidden), jnp.float32),
            pltpu.SemaphoreType.DMA((2,)),
            pltpu.SemaphoreType.DMA((max(n_col - 1, 1), n_a)),
            pltpu.SemaphoreType.DMA,
            pltpu.SemaphoreType.DMA((2, n_w)),
            pltpu.SemaphoreType.DMA,
            pltpu.SemaphoreType.DMA((2,)),
            pltpu.SemaphoreType.REGULAR,
            pltpu.VMEM((cuts[-1], width), jnp.bfloat16),
            pltpu.SemaphoreType.DMA,
            pltpu.SemaphoreType.DMA,
        ],
        compiler_params=pltpu.CompilerParams(collective_id=0, has_side_effects=True, vmem_limit_bytes=60000000),
        cost_estimate=pl.CostEstimate(
            flops=2 * tokens * width * n_col * hidden,
            bytes_accessed=2 * (act_tiles.size + up_tiles.size + tokens * hidden),
            transcendentals=tokens * hidden,
        ),
        name="gather_up_silu",
    )(act_tiles, up_tiles)


def solution(mesh):
    return jax.shard_map(
        functools.partial(body, mesh.shape["row"], mesh.shape["col"]),
        mesh=mesh,
        in_specs=(P("row", "col"), P("row", "col")),
        out_specs=P("row", "col"),
        check_vma=False,
    )
```

```python
import functools

import jax
import jax.numpy as jnp
from jax import lax
from jax.experimental import pallas as pl
from jax.experimental.pallas import tpu as pltpu
from jax.sharding import PartitionSpec as P

MESH = pl.DeviceIdType.MESH


def pieces_of(rows, wanted, multiple):
    return max(n for n in range(1, wanted + 1) if rows % (n * multiple) == 0)


def pieces_uneven(rows, shares, multiple):
    unit = rows // sum(shares)
    return [n * unit for n in shares] if unit * sum(shares) == rows and unit % multiple == 0 else [rows]


def nth_source(n_col, c, t):
    last = n_col - 1
    short = jnp.minimum(c, last - c)
    toward = jnp.where(last - c >= c, 1, -1)
    near_step = t // 2 + 1
    near_sign = toward * (1 - 2 * lax.rem(t, 2))
    return jnp.where(t < 2 * short, c + near_sign * near_step, c + toward * (t - short + 1))


def product_of(n_col, c, acts, weights, source, rows):
    width, (depth, hidden) = acts.shape[2], weights.shape[1:]
    per = width // depth
    at = lax.rem(source - c + n_col, n_col)
    held = weights[pl.ds(at * per, per)].reshape(width, hidden)
    return jnp.dot(acts[source, rows, :], held, preferred_element_type=jnp.float32)


def finish(n_col, start, ready, acts, weights, total, out, tail, sems):
    c = lax.axis_index("col")
    size = tail.shape[0]
    rows = pl.ds(start, size)
    head = pl.ds(0, start)
    first = pltpu.make_async_copy(ready.at[head], out.at[head], sems.at[0])
    if start:
        first.start()
    pre = total[rows, :] + product_of(n_col, c, acts, weights, nth_source(n_col, c, n_col - 2), rows)
    tail[...] = (pre / (1.0 + jnp.exp(-pre))).astype(out.dtype)
    second = pltpu.make_async_copy(tail, out.at[rows], sems.at[1])
    second.start()
    if start:
        first.wait()
    second.wait()


def kernel(grid, counts, a_hbm, w_hbm, out, acts, weights, total, send_a, recv_a, send_w, recv_w, share_w, local_sem, go, held, send_h, recv_h):
    n_y, n_x, n_col = grid
    n_a, n_w = counts
    n_row = 2 * n_y * n_x
    tokens, width = acts.shape[1:]
    depth, hidden = weights.shape[1:]
    per = width // depth
    row_w = depth // n_w
    starts_a = [sum(n_a[:k]) for k in range(len(n_a))]
    sizes_a, n_a = n_a, len(n_a)

    r, c = lax.axis_index("row"), lax.axis_index("col")
    core = lax.rem(r, 2)
    x = lax.rem(r // 2, n_x)
    y = r // (2 * n_x)
    last = n_col - 1

    def row_of(dy, dx, other_core=False):
        which = 1 - core if other_core else core
        return (lax.rem(y + dy, n_y) * n_x + lax.rem(x + dx, n_x)) * 2 + which

    pair = row_of(0, 0, True)
    peers_x = [(0, dx) for dx in range(1, n_x)]
    peers_y = [(dy, 0) for dy in range(1, n_y)]
    diagonal = [(dy, dx) for dy in range(1, n_y) for dx in range(1, n_x)]
    near = [row_of(*p) for p in peers_x + peers_y]
    far = [row_of(*p) for p in diagonal]
    row_peers = near + [pair]

    helpers = []
    if n_a > 2 and n_col > 1:
        helpers += [(3, n_a - 2)] if n_x > 1 else []
        helpers += [(2 * n_x + 1, n_a - 1)] if n_y > 1 else []

    def weight_at(source, owner, k):
        rel = lax.rem(source - owner + n_row, n_row)
        return weights.at[rel, pl.ds(k * row_w, row_w)]

    def weight_copy(source, to, recv, k, own=False):
        return pltpu.make_async_remote_copy(
            src_ref=w_hbm.at[pl.ds(k * row_w, row_w)] if own else weight_at(source, r, k),
            dst_ref=weight_at(source, to, k),
            send_sem=send_w,
            recv_sem=recv,
            device_id=(to, c),
            device_id_type=MESH,
        )

    def act_copy(source, side, k, own=False, arrives=False):
        to = c if arrives else c + 2 * side - 1
        rows = pl.ds(starts_a[k], sizes_a[k])
        return pltpu.make_async_remote_copy(
            src_ref=a_hbm.at[rows] if own else acts.at[source, rows],
            dst_ref=acts.at[source, rows],
            send_sem=send_a.at[side],
            recv_sem=recv_a.at[lax.rem(source - to + n_col, n_col) - 1, k],
            device_id=(r, to),
            device_id_type=MESH,
        )

    def held_copy(src, dst, to, send, recv):
        return pltpu.make_async_remote_copy(
            src_ref=src, dst_ref=dst, send_sem=send, recv_sem=recv, device_id=to, device_id_type=MESH
        )

    def wait_acts(source, k):
        act_copy(source, 0, k, arrives=True).wait_recv()

    def filled(ref, sem):
        pltpu.make_async_copy(ref, ref, sem).wait()

    barrier = pltpu.get_barrier_semaphore()

    def greet(to):
        pl.semaphore_signal(barrier, inc=1, device_id=to, device_id_type=MESH)

    def tell(to):
        pl.semaphore_signal(go, inc=1, device_id=to, device_id_type=MESH)

    early = c == 1

    @pl.when(jnp.logical_and(c < last, c != 0))
    def _():
        greet((r, c + 1))

    @pl.when(jnp.logical_and(c > 0, c != 2))
    def _():
        greet((r, c - 1))

    @pl.when(jnp.logical_and(c == 0, c < last))
    def _():
        greet((r, c + 1))

    @pl.when(jnp.logical_not(early))
    def _():
        for to in row_peers:
            greet((to, c))

    for helper, _ in helpers:
        @pl.when(jnp.logical_and(c == 0, r == 0))
        def _():
            greet((helper, 0))

        @pl.when(jnp.logical_and(c == 0, r == helper))
        def _():
            greet((0, 0))

    helped = jnp.where(r == 0, len(helpers), sum((jnp.where(r == helper, 1, 0) for helper, _ in helpers), 0))
    helped = jnp.where(c == 0, helped, 0)

    own_a = pltpu.make_async_copy(a_hbm, acts.at[c], local_sem.at[0])
    own_w = pltpu.make_async_copy(w_hbm, weights.at[0], local_sem.at[1])
    own_a.start()
    own_w.start()

    def own_acts(side):
        for k in range(n_a):
            act_copy(c, side, k, True).start()

    @pl.when(early)
    def _():
        pl.semaphore_wait(barrier, 1)
        for k in range(n_a):
            if k in [taken for _, taken in helpers]:
                pl.when(r != 0)(act_copy(c, 0, k, True).start)
            else:
                act_copy(c, 0, k, True).start()
        pl.semaphore_wait(go, 2 if n_col > 2 else 1)

        @pl.when(r == 0)
        def _():
            for helper, k in helpers:
                held_copy(a_hbm.at[pl.ds(starts_a[k], sizes_a[k])], held, (helper, 1), send_a.at[0], recv_h).start()

    @pl.when(jnp.logical_not(early))
    def _():
        beside = jnp.where(c > 0, 1, 0) + jnp.where(c < last, 1, 0)
        pl.semaphore_wait(barrier, len(row_peers) + beside + helped)

        @pl.when(c > 0)
        def _():
            own_acts(0)

        @pl.when(c == 2)
        def _():
            tell((r, c - 1))

    @pl.when(jnp.logical_and(c == 0, c < last))
    def _():
        for to in row_peers:
            tell((to, c))
        for helper, _ in helpers:
            pl.when(r == helper)(functools.partial(tell, (0, c)))

    @pl.when(c < last)
    def _():
        own_acts(1)

    for k in range(n_w):
        for to in near:
            weight_copy(r, to, recv_w.at[0, k], k, True).start()
        weight_copy(r, pair, share_w, k, True).start()

    @pl.when(jnp.logical_and(c == 0, c < last))
    def _():
        pl.semaphore_wait(go, len(row_peers) + jnp.where(r == 0, len(helpers), 0))
        tell((r, c + 1))

    def first_weights(k):
        filled(weights.at[pl.ds(0, len(near)), pl.ds(0, row_w)], recv_w.at[0, k])
        for dy, dx in diagonal:
            @pl.when(core == 0)
            def _():
                weight_copy(row_of(dy, 0), row_of(0, dx), recv_w.at[1, k], k).start()

            @pl.when(core == 1)
            def _():
                weight_copy(row_of(0, dx), row_of(dy, 0), recv_w.at[1, k], k).start()
        for source in near:
            weight_copy(source, pair, share_w, k).start()

    def far_weights(k):
        filled(weights.at[pl.ds(0, len(far)), pl.ds(0, row_w)], recv_w.at[1, k])
        for source in far:
            weight_copy(source, pair, share_w, k).start()

    source_at = functools.partial(nth_source, n_col, c)
    inner = jnp.logical_and(c > 0, c < last)

    def pass_acts(t, k):
        source = source_at(t)
        wait_acts(source, k)

        @pl.when(source < c)
        def _():
            act_copy(source, 1, k).start()

        @pl.when(source > c)
        def _():
            act_copy(source, 0, k).start()

    def help_out():
        for helper, k in helpers:
            @pl.when(jnp.logical_and(c == 1, r == helper))
            def _():
                filled(held, recv_h)
                held_copy(held, held, (r, 0), send_h, recv_h).start()

    def help_in():
        for helper, k in helpers:
            @pl.when(jnp.logical_and(c == 0, r == helper))
            def _():
                filled(held, recv_h)
                there = acts.at[1, pl.ds(starts_a[k], sizes_a[k])]
                held_copy(held, there, (0, 0), send_h, recv_a.at[0, k]).start()

    events = [(0.4 * tokens * width, "out", 0, 0), (1.1 * tokens * width, "in", 0, 0)]
    w_time, w_lag = row_w * hidden, tokens * width / 10
    for t in range(last):
        for k in range(n_a):
            events.append(((t // 2 * tokens + starts_a[k] + sizes_a[k]) * width, "a", t, k))
    for k in range(n_w):
        events.append(((k + 1) * w_time * (n_x + n_y - 2) / 2 + w_lag, "near", 0, k))
        events.append(((k + 2) * w_time * (n_x + n_y - 2) / 2 + w_time + w_lag, "far", 0, k))
    for _, kind, t, k in sorted(events):
        if kind == "a":
            pl.when(inner)(functools.partial(pass_acts, t, k))
        elif kind == "out":
            help_out()
        elif kind == "in":
            help_in()
        elif kind == "near":
            first_weights(k)
        elif diagonal:
            far_weights(k)
    filled(weights.at[pl.ds(0, n_row // 2)], share_w)
    own_w.wait()
    own_a.wait()

    product = functools.partial(product_of, n_col, c, acts, weights)

    every = pl.ds(0, tokens)
    total[...] = product(c, every)

    @pl.loop(0, last - 1)
    def _(t):
        source = source_at(t)

        @pl.when(jnp.logical_not(inner))
        def _():
            for k in range(n_a):
                wait_acts(source, k)

        total[...] += product(source, every)

    final = source_at(last - 1)

    for k in range(n_a):
        rows = pl.ds(starts_a[k], sizes_a[k])

        pl.when(jnp.logical_not(inner))(functools.partial(wait_acts, final, k))

        if k == n_a - 1:
            break
        pre = total[rows, :] + product(final, rows)
        out[rows, :] = (pre / (1.0 + jnp.exp(-pre))).astype(out.dtype)

    for n in range(1, n_col):
        pl.when(jnp.logical_and(c < last, c + 1 == n))(functools.partial(filled, acts.at[pl.ds(0, n)], send_a.at[1]))
        pl.when(jnp.logical_and(c > 0, n_col - c == n))(functools.partial(filled, acts.at[pl.ds(0, n)], send_a.at[0]))
    for helper, _ in helpers:
        pl.when(jnp.logical_and(c < 2, r == helper))(functools.partial(filled, held, send_h))
    filled(weights.at[pl.ds(0, n_row - 1)], send_w)


def body(n_row, n_col, act_tiles, up_tiles):
    tokens, width = act_tiles.shape
    depth, hidden = up_tiles.shape
    chips = n_row // 2
    n_x = max(n for n in range(1, chips + 1) if chips % n == 0 and n * n <= chips)
    n_y = chips // n_x
    cuts, n_w = pieces_uneven(tokens, (2, 4, 1, 1), 16), pieces_of(depth, 2, 16)
    n_a = len(cuts)
    held = pl.pallas_call(
        functools.partial(kernel, (n_y, n_x, n_col), (cuts, n_w)),
        out_shape=(
            pltpu.VMEM((tokens, hidden), jnp.bfloat16),
            pltpu.VMEM((n_col, tokens, width), jnp.bfloat16),
            pltpu.VMEM((n_row, depth, hidden), jnp.bfloat16),
            pltpu.VMEM((tokens, hidden), jnp.float32),
        ),
        in_specs=[pl.BlockSpec(memory_space=pltpu.HBM)] * 2,
        out_specs=(pl.BlockSpec(memory_space=pltpu.VMEM),) * 4,
        scratch_shapes=[
            pltpu.SemaphoreType.DMA((2,)),
            pltpu.SemaphoreType.DMA((max(n_col - 1, 1), n_a)),
            pltpu.SemaphoreType.DMA,
            pltpu.SemaphoreType.DMA((2, n_w)),
            pltpu.SemaphoreType.DMA,
            pltpu.SemaphoreType.DMA((2,)),
            pltpu.SemaphoreType.REGULAR,
            pltpu.VMEM((cuts[-1], width), jnp.bfloat16),
            pltpu.SemaphoreType.DMA,
            pltpu.SemaphoreType.DMA,
        ],
        compiler_params=pltpu.CompilerParams(collective_id=0, has_side_effects=True, vmem_limit_bytes=8000000),
        cost_estimate=pl.CostEstimate(
            flops=2 * tokens * width * n_col * hidden,
            bytes_accessed=2 * (act_tiles.size + up_tiles.size + tokens * hidden),
            transcendentals=tokens * hidden,
        ),
        name="gather_up_silu",
    )(*[pltpu.with_memory_space_constraint(a, pltpu.HBM) for a in (act_tiles, up_tiles)])
    return pl.pallas_call(
        functools.partial(finish, n_col, tokens - cuts[-1]),
        out_shape=jax.ShapeDtypeStruct((tokens, hidden), jnp.bfloat16),
        in_specs=[pl.BlockSpec(memory_space=pltpu.VMEM)] * 4,
        out_specs=pl.BlockSpec(memory_space=pltpu.HBM),
        scratch_shapes=[pltpu.VMEM((cuts[-1], hidden), jnp.bfloat16), pltpu.SemaphoreType.DMA((2,))],
        compiler_params=pltpu.CompilerParams(vmem_limit_bytes=8000000),
        name="last_rows",
    )(*[pltpu.with_memory_space_constraint(a, pltpu.VMEM) for a in held])


def solution(mesh):
    return jax.shard_map(
        functools.partial(body, mesh.shape["row"], mesh.shape["col"]),
        mesh=mesh,
        in_specs=(P("row", "col"), P("row", "col")),
        out_specs=P("row", "col"),
        check_vma=False,
    )
```

```python
import functools

import jax
import jax.numpy as jnp
from jax import lax
from jax.experimental import pallas as pl
from jax.experimental.pallas import tpu as pltpu
from jax.sharding import PartitionSpec as P

MESH = pl.DeviceIdType.MESH


def pieces_of(rows, wanted, multiple):
    return max(n for n in range(1, wanted + 1) if rows % (n * multiple) == 0)


def pieces_uneven(rows, shares, multiple):
    unit = rows // sum(shares)
    return [n * unit for n in shares] if unit * sum(shares) == rows and unit % multiple == 0 else [rows]


def nth_source(n_col, c, t):
    last = n_col - 1
    short = jnp.minimum(c, last - c)
    toward = jnp.where(last - c >= c, 1, -1)
    near_step = t // 2 + 1
    near_sign = toward * (1 - 2 * lax.rem(t, 2))
    return jnp.where(t < 2 * short, c + near_sign * near_step, c + toward * (t - short + 1))


def product_of(n_col, c, acts, weights, source, rows):
    width, (depth, hidden) = acts.shape[2], weights.shape[1:]
    per = width // depth
    at = lax.rem(source - c + n_col, n_col)
    held = weights[pl.ds(at * per, per)].reshape(width, hidden)
    return jnp.dot(acts[source, rows, :], held, preferred_element_type=jnp.float32)


def finish(n_col, start, ready, acts, weights, total, out, tail, sems):
    c = lax.axis_index("col")
    size = tail.shape[0]
    rows = pl.ds(start, size)
    head = pl.ds(0, start)
    first = pltpu.make_async_copy(ready.at[head], out.at[head], sems.at[0])
    if start:
        first.start()
    pre = total[rows, :] + product_of(n_col, c, acts, weights, nth_source(n_col, c, n_col - 2), rows)
    tail[...] = (pre / (1.0 + jnp.exp(-pre))).astype(out.dtype)
    second = pltpu.make_async_copy(tail, out.at[rows], sems.at[1])
    second.start()
    if start:
        first.wait()
    second.wait()


def kernel(grid, counts, a_hbm, w_hbm, out, acts, weights, total, send_a, recv_a, send_w, recv_w, share_w, local_sem, go, held, send_h, recv_h):
    n_y, n_x, n_col = grid
    n_a, n_w = counts
    n_row = 2 * n_y * n_x
    tokens, width = acts.shape[1:]
    depth, hidden = weights.shape[1:]
    per = width // depth
    row_w = depth // n_w
    starts_a = [sum(n_a[:k]) for k in range(len(n_a))]
    sizes_a, n_a = n_a, len(n_a)

    r, c = lax.axis_index("row"), lax.axis_index("col")
    core = lax.rem(r, 2)
    x = lax.rem(r // 2, n_x)
    y = r // (2 * n_x)
    last = n_col - 1

    def row_of(dy, dx, other_core=False):
        which = 1 - core if other_core else core
        return (lax.rem(y + dy, n_y) * n_x + lax.rem(x + dx, n_x)) * 2 + which

    pair = row_of(0, 0, True)
    peers_x = [(0, dx) for dx in range(1, n_x)]
    peers_y = [(dy, 0) for dy in range(1, n_y)]
    diagonal = [(dy, dx) for dy in range(1, n_y) for dx in range(1, n_x)]
    near = [row_of(*p) for p in peers_x + peers_y]
    far = [row_of(*p) for p in diagonal]
    row_peers = near + [pair]

    helpers = []
    if n_a > 3 and n_col > 1:
        helpers += [(3, n_a - 3)] if n_x > 1 else []
        helpers += [(2 * n_x + 1, n_a - 2)] if n_y > 1 else []
        helpers += [(2 * n_x + 3, n_a - 1)] if n_x > 1 and n_y > 1 else []

    def weight_at(source, owner, k):
        rel = lax.rem(source - owner + n_row, n_row)
        return weights.at[rel, pl.ds(k * row_w, row_w)]

    def weight_copy(source, to, recv, k, own=False):
        return pltpu.make_async_remote_copy(
            src_ref=w_hbm.at[pl.ds(k * row_w, row_w)] if own else weight_at(source, r, k),
            dst_ref=weight_at(source, to, k),
            send_sem=send_w,
            recv_sem=recv,
            device_id=(to, c),
            device_id_type=MESH,
        )

    def act_copy(source, side, k, own=False, arrives=False):
        to = c if arrives else c + 2 * side - 1
        rows = pl.ds(starts_a[k], sizes_a[k])
        return pltpu.make_async_remote_copy(
            src_ref=a_hbm.at[rows] if own else acts.at[source, rows],
            dst_ref=acts.at[source, rows],
            send_sem=send_a.at[side],
            recv_sem=recv_a.at[lax.rem(source - to + n_col, n_col) - 1, k],
            device_id=(r, to),
            device_id_type=MESH,
        )

    def held_copy(src, dst, to, send, recv):
        return pltpu.make_async_remote_copy(
            src_ref=src, dst_ref=dst, send_sem=send, recv_sem=recv, device_id=to, device_id_type=MESH
        )

    def wait_acts(source, k):
        act_copy(source, 0, k, arrives=True).wait_recv()

    def filled(ref, sem):
        pltpu.make_async_copy(ref, ref, sem).wait()

    barrier = pltpu.get_barrier_semaphore()

    def greet(to):
        pl.semaphore_signal(barrier, inc=1, device_id=to, device_id_type=MESH)

    def tell(to):
        pl.semaphore_signal(go, inc=1, device_id=to, device_id_type=MESH)

    early = c == 1

    @pl.when(jnp.logical_and(c < last, c != 0))
    def _():
        greet((r, c + 1))

    @pl.when(jnp.logical_and(c > 0, c != 2))
    def _():
        greet((r, c - 1))

    @pl.when(jnp.logical_and(c == 0, c < last))
    def _():
        greet((r, c + 1))

    @pl.when(jnp.logical_not(early))
    def _():
        for to in row_peers:
            greet((to, c))

    for helper, _ in helpers:
        @pl.when(jnp.logical_and(c == 0, r == 0))
        def _():
            greet((helper, 0))

        @pl.when(jnp.logical_and(c == 0, r == helper))
        def _():
            greet((0, 0))

    helped = jnp.where(r == 0, len(helpers), sum((jnp.where(r == helper, 1, 0) for helper, _ in helpers), 0))
    helped = jnp.where(c == 0, helped, 0)

    own_a = pltpu.make_async_copy(a_hbm, acts.at[c], local_sem.at[0])
    own_w = pltpu.make_async_copy(w_hbm, weights.at[0], local_sem.at[1])
    own_a.start()
    own_w.start()

    def own_acts(side):
        for k in range(n_a):
            act_copy(c, side, k, True).start()

    @pl.when(early)
    def _():
        pl.semaphore_wait(barrier, 1)
        for k in range(n_a):
            if k in [taken for _, taken in helpers]:
                pl.when(r != 0)(act_copy(c, 0, k, True).start)
            else:
                act_copy(c, 0, k, True).start()
        pl.semaphore_wait(go, 2 if n_col > 2 else 1)

        @pl.when(r == 0)
        def _():
            for helper, k in helpers:
                held_copy(a_hbm.at[pl.ds(starts_a[k], sizes_a[k])], held, (helper, 1), send_a.at[0], recv_h).start()

    @pl.when(jnp.logical_not(early))
    def _():
        beside = jnp.where(c > 0, 1, 0) + jnp.where(c < last, 1, 0)
        pl.semaphore_wait(barrier, len(row_peers) + beside + helped)

        @pl.when(c > 0)
        def _():
            own_acts(0)

        @pl.when(c == 2)
        def _():
            tell((r, c - 1))

    @pl.when(jnp.logical_and(c == 0, c < last))
    def _():
        for to in row_peers:
            tell((to, c))
        for helper, _ in helpers:
            pl.when(r == helper)(functools.partial(tell, (0, c)))

    @pl.when(c < last)
    def _():
        own_acts(1)

    for k in range(n_w):
        for to in near:
            weight_copy(r, to, recv_w.at[0, k], k, True).start()
        weight_copy(r, pair, share_w, k, True).start()

    @pl.when(jnp.logical_and(c == 0, c < last))
    def _():
        pl.semaphore_wait(go, len(row_peers) + jnp.where(r == 0, len(helpers), 0))
        tell((r, c + 1))

    def first_weights(k):
        filled(weights.at[pl.ds(0, len(near)), pl.ds(0, row_w)], recv_w.at[0, k])
        for dy, dx in diagonal:
            @pl.when(core == 0)
            def _():
                weight_copy(row_of(dy, 0), row_of(0, dx), recv_w.at[1, k], k).start()

            @pl.when(core == 1)
            def _():
                weight_copy(row_of(0, dx), row_of(dy, 0), recv_w.at[1, k], k).start()
        for source in near:
            weight_copy(source, pair, share_w, k).start()

    def far_weights(k):
        filled(weights.at[pl.ds(0, len(far)), pl.ds(0, row_w)], recv_w.at[1, k])
        for source in far:
            weight_copy(source, pair, share_w, k).start()

    source_at = functools.partial(nth_source, n_col, c)
    inner = jnp.logical_and(c > 0, c < last)

    def pass_acts(t, k):
        source = source_at(t)
        wait_acts(source, k)

        @pl.when(source < c)
        def _():
            act_copy(source, 1, k).start()

        @pl.when(source > c)
        def _():
            act_copy(source, 0, k).start()

    def help_out():
        for helper, k in helpers:
            @pl.when(jnp.logical_and(c == 1, r == helper))
            def _():
                filled(held, recv_h)
                held_copy(held, held, (r, 0), send_h, recv_h).start()

    def help_in():
        for helper, k in helpers:
            @pl.when(jnp.logical_and(c == 0, r == helper))
            def _():
                filled(held, recv_h)
                there = acts.at[1, pl.ds(starts_a[k], sizes_a[k])]
                held_copy(held, there, (0, 0), send_h, recv_a.at[0, k]).start()

    events = [(0.4 * tokens * width, "out", 0, 0), (1.1 * tokens * width, "in", 0, 0)]
    w_time, w_lag = row_w * hidden, tokens * width / 10
    for t in range(last):
        for k in range(n_a):
            events.append(((t // 2 * tokens + starts_a[k] + sizes_a[k]) * width, "a", t, k))
    for k in range(n_w):
        events.append(((k + 1) * w_time * (n_x + n_y - 2) / 2 + w_lag, "near", 0, k))
        events.append(((k + 2) * w_time * (n_x + n_y - 2) / 2 + w_time + w_lag, "far", 0, k))
    for _, kind, t, k in sorted(events):
        if kind == "a":
            pl.when(inner)(functools.partial(pass_acts, t, k))
        elif kind == "out":
            help_out()
        elif kind == "in":
            help_in()
        elif kind == "near":
            first_weights(k)
        elif diagonal:
            far_weights(k)
    filled(weights.at[pl.ds(0, n_row // 2)], share_w)
    own_w.wait()
    own_a.wait()

    product = functools.partial(product_of, n_col, c, acts, weights)

    every = pl.ds(0, tokens)
    total[...] = product(c, every)

    @pl.loop(0, last - 1)
    def _(t):
        source = source_at(t)

        @pl.when(jnp.logical_not(inner))
        def _():
            for k in range(n_a):
                wait_acts(source, k)

        total[...] += product(source, every)

    final = source_at(last - 1)

    for k in range(n_a):
        rows = pl.ds(starts_a[k], sizes_a[k])

        pl.when(jnp.logical_not(inner))(functools.partial(wait_acts, final, k))

        if k == n_a - 1:
            break
        pre = total[rows, :] + product(final, rows)
        out[rows, :] = (pre / (1.0 + jnp.exp(-pre))).astype(out.dtype)

    for n in range(1, n_col):
        pl.when(jnp.logical_and(c < last, c + 1 == n))(functools.partial(filled, acts.at[pl.ds(0, n)], send_a.at[1]))
        pl.when(jnp.logical_and(c > 0, n_col - c == n))(functools.partial(filled, acts.at[pl.ds(0, n)], send_a.at[0]))
    for helper, _ in helpers:
        pl.when(jnp.logical_and(c < 2, r == helper))(functools.partial(filled, held, send_h))
    filled(weights.at[pl.ds(0, n_row - 1)], send_w)


def body(n_row, n_col, act_tiles, up_tiles):
    tokens, width = act_tiles.shape
    depth, hidden = up_tiles.shape
    chips = n_row // 2
    n_x = max(n for n in range(1, chips + 1) if chips % n == 0 and n * n <= chips)
    n_y = chips // n_x
    cuts, n_w = pieces_uneven(tokens, (6, 12, 2, 2, 2), 16), pieces_of(depth, 2, 16)
    n_a = len(cuts)
    held = pl.pallas_call(
        functools.partial(kernel, (n_y, n_x, n_col), (cuts, n_w)),
        out_shape=(
            pltpu.VMEM((tokens, hidden), jnp.bfloat16),
            pltpu.VMEM((n_col, tokens, width), jnp.bfloat16),
            pltpu.VMEM((n_row, depth, hidden), jnp.bfloat16),
            pltpu.VMEM((tokens, hidden), jnp.float32),
        ),
        in_specs=[pl.BlockSpec(memory_space=pltpu.HBM)] * 2,
        out_specs=(pl.BlockSpec(memory_space=pltpu.VMEM),) * 4,
        scratch_shapes=[
            pltpu.SemaphoreType.DMA((2,)),
            pltpu.SemaphoreType.DMA((max(n_col - 1, 1), n_a)),
            pltpu.SemaphoreType.DMA,
            pltpu.SemaphoreType.DMA((2, n_w)),
            pltpu.SemaphoreType.DMA,
            pltpu.SemaphoreType.DMA((2,)),
            pltpu.SemaphoreType.REGULAR,
            pltpu.VMEM((cuts[-1], width), jnp.bfloat16),
            pltpu.SemaphoreType.DMA,
            pltpu.SemaphoreType.DMA,
        ],
        compiler_params=pltpu.CompilerParams(collective_id=0, has_side_effects=True, vmem_limit_bytes=8000000),
        cost_estimate=pl.CostEstimate(
            flops=2 * tokens * width * n_col * hidden,
            bytes_accessed=2 * (act_tiles.size + up_tiles.size + tokens * hidden),
            transcendentals=tokens * hidden,
        ),
        name="gather_up_silu",
    )(*[pltpu.with_memory_space_constraint(a, pltpu.HBM) for a in (act_tiles, up_tiles)])
    return pl.pallas_call(
        functools.partial(finish, n_col, tokens - cuts[-1]),
        out_shape=jax.ShapeDtypeStruct((tokens, hidden), jnp.bfloat16),
        in_specs=[pl.BlockSpec(memory_space=pltpu.VMEM)] * 4,
        out_specs=pl.BlockSpec(memory_space=pltpu.HBM),
        scratch_shapes=[pltpu.VMEM((cuts[-1], hidden), jnp.bfloat16), pltpu.SemaphoreType.DMA((2,))],
        compiler_params=pltpu.CompilerParams(vmem_limit_bytes=8000000),
        name="last_rows",
    )(*[pltpu.with_memory_space_constraint(a, pltpu.VMEM) for a in held])


def solution(mesh):
    return jax.shard_map(
        functools.partial(body, mesh.shape["row"], mesh.shape["col"]),
        mesh=mesh,
        in_specs=(P("row", "col"), P("row", "col")),
        out_specs=P("row", "col"),
        check_vma=False,
    )
```

```python
import functools

import jax
import jax.numpy as jnp
from jax import lax
from jax.experimental import pallas as pl
from jax.experimental.pallas import tpu as pltpu
from jax.sharding import PartitionSpec as P

MESH = pl.DeviceIdType.MESH


def pieces_of(rows, wanted, multiple):
    return max(n for n in range(1, wanted + 1) if rows % (n * multiple) == 0)


def pieces_uneven(rows, shares, multiple):
    unit = rows // sum(shares)
    return [n * unit for n in shares] if unit * sum(shares) == rows and unit % multiple == 0 else [rows]


def nth_source(n_col, c, t):
    last = n_col - 1
    short = jnp.minimum(c, last - c)
    toward = jnp.where(last - c >= c, 1, -1)
    near_step = t // 2 + 1
    near_sign = toward * (1 - 2 * lax.rem(t, 2))
    return jnp.where(t < 2 * short, c + near_sign * near_step, c + toward * (t - short + 1))


def product_of(n_col, c, acts, weights, source, rows):
    width, (depth, hidden) = acts.shape[2], weights.shape[1:]
    per = width // depth
    at = lax.rem(source - c + n_col, n_col)
    held = weights[pl.ds(at * per, per)].reshape(width, hidden)
    return jnp.dot(acts[source, rows, :], held, preferred_element_type=jnp.float32)


def finish(n_col, start, ready, acts, weights, total, out, tail, sems):
    c = lax.axis_index("col")
    size = tail.shape[0]
    rows = pl.ds(start, size)
    head = pl.ds(0, start)
    first = pltpu.make_async_copy(ready.at[head], out.at[head], sems.at[0])
    if start:
        first.start()
    pre = total[rows, :] + product_of(n_col, c, acts, weights, nth_source(n_col, c, n_col - 2), rows)
    tail[...] = (pre / (1.0 + jnp.exp(-pre))).astype(out.dtype)
    second = pltpu.make_async_copy(tail, out.at[rows], sems.at[1])
    second.start()
    if start:
        first.wait()
    second.wait()


def kernel(grid, counts, a_hbm, w_hbm, out, acts, weights, total, send_a, recv_a, send_w, recv_w, share_w, local_sem, go, held, send_h, recv_h):
    n_y, n_x, n_col = grid
    n_a, n_w = counts
    n_row = 2 * n_y * n_x
    tokens, width = acts.shape[1:]
    depth, hidden = weights.shape[1:]
    per = width // depth
    row_w = depth // n_w
    starts_a = [sum(n_a[:k]) for k in range(len(n_a))]
    sizes_a, n_a = n_a, len(n_a)

    r, c = lax.axis_index("row"), lax.axis_index("col")
    core = lax.rem(r, 2)
    x = lax.rem(r // 2, n_x)
    y = r // (2 * n_x)
    last = n_col - 1

    def row_of(dy, dx, other_core=False):
        which = 1 - core if other_core else core
        return (lax.rem(y + dy, n_y) * n_x + lax.rem(x + dx, n_x)) * 2 + which

    pair = row_of(0, 0, True)
    peers_x = [(0, dx) for dx in range(1, n_x)]
    peers_y = [(dy, 0) for dy in range(1, n_y)]
    diagonal = [(dy, dx) for dy in range(1, n_y) for dx in range(1, n_x)]
    near = [row_of(*p) for p in peers_x + peers_y]
    far = [row_of(*p) for p in diagonal]
    row_peers = near + [pair]

    helpers = []
    if n_a > 3 and n_col > 1:
        helpers += [(3, n_a - 3)] if n_x > 1 else []
        helpers += [(2 * n_x + 1, n_a - 2)] if n_y > 1 else []
        helpers += [(2 * n_x + 3, n_a - 1)] if n_x > 1 and n_y > 1 else []

    def weight_at(source, owner, k):
        rel = lax.rem(source - owner + n_row, n_row)
        return weights.at[rel, pl.ds(k * row_w, row_w)]

    def weight_copy(source, to, recv, k, own=False):
        return pltpu.make_async_remote_copy(
            src_ref=w_hbm.at[pl.ds(k * row_w, row_w)] if own else weight_at(source, r, k),
            dst_ref=weight_at(source, to, k),
            send_sem=send_w,
            recv_sem=recv,
            device_id=(to, c),
            device_id_type=MESH,
        )

    def act_copy(source, side, k, own=False, arrives=False):
        to = c if arrives else c + 2 * side - 1
        rows = pl.ds(starts_a[k], sizes_a[k])
        return pltpu.make_async_remote_copy(
            src_ref=a_hbm.at[rows] if own else acts.at[source, rows],
            dst_ref=acts.at[source, rows],
            send_sem=send_a.at[side],
            recv_sem=recv_a.at[lax.rem(source - to + n_col, n_col) - 1, k],
            device_id=(r, to),
            device_id_type=MESH,
        )

    def held_copy(src, dst, to, send, recv):
        return pltpu.make_async_remote_copy(
            src_ref=src, dst_ref=dst, send_sem=send, recv_sem=recv, device_id=to, device_id_type=MESH
        )

    def wait_acts(source, k):
        act_copy(source, 0, k, arrives=True).wait_recv()

    def filled(ref, sem):
        pltpu.make_async_copy(ref, ref, sem).wait()

    barrier = pltpu.get_barrier_semaphore()

    def greet(to):
        pl.semaphore_signal(barrier, inc=1, device_id=to, device_id_type=MESH)

    def tell(to):
        pl.semaphore_signal(go, inc=1, device_id=to, device_id_type=MESH)

    early = c == 1

    @pl.when(jnp.logical_and(c < last, c != 0))
    def _():
        greet((r, c + 1))

    @pl.when(jnp.logical_and(c > 0, c != 2))
    def _():
        greet((r, c - 1))

    @pl.when(jnp.logical_and(c == 0, c < last))
    def _():
        greet((r, c + 1))

    @pl.when(jnp.logical_not(early))
    def _():
        for to in row_peers:
            greet((to, c))

    for helper, _ in helpers:
        @pl.when(jnp.logical_and(c == 0, r == 0))
        def _():
            greet((helper, 0))

        @pl.when(jnp.logical_and(c == 0, r == helper))
        def _():
            greet((0, 0))

    helped = jnp.where(r == 0, len(helpers), sum((jnp.where(r == helper, 1, 0) for helper, _ in helpers), 0))
    helped = jnp.where(c == 0, helped, 0)

    own_a = pltpu.make_async_copy(a_hbm, acts.at[c], local_sem)
    own_w = pltpu.make_async_copy(w_hbm, weights.at[0], share_w)
    own_a.start()
    own_w.start()

    def own_acts(side):
        for k in range(n_a):
            act_copy(c, side, k, True).start()

    @pl.when(early)
    def _():
        pl.semaphore_wait(barrier, 1)
        for k in range(n_a):
            if k in [taken for _, taken in helpers]:
                pl.when(r != 0)(act_copy(c, 0, k, True).start)
            else:
                act_copy(c, 0, k, True).start()
        pl.semaphore_wait(go, 2 if n_col > 2 else 1)

        @pl.when(r == 0)
        def _():
            for helper, k in helpers:
                held_copy(a_hbm.at[pl.ds(starts_a[k], sizes_a[k])], held, (helper, 1), send_a.at[0], recv_h).start()

    @pl.when(jnp.logical_not(early))
    def _():
        beside = jnp.where(c > 0, 1, 0) + jnp.where(c < last, 1, 0)
        pl.semaphore_wait(barrier, len(row_peers) + beside + helped)

        @pl.when(c > 0)
        def _():
            own_acts(0)

        @pl.when(c == 2)
        def _():
            tell((r, c - 1))

    @pl.when(jnp.logical_and(c == 0, c < last))
    def _():
        for to in row_peers:
            tell((to, c))
        for helper, _ in helpers:
            pl.when(r == helper)(functools.partial(tell, (0, c)))

    @pl.when(c < last)
    def _():
        own_acts(1)

    for k in range(n_w):
        for to in near:
            weight_copy(r, to, recv_w.at[0, k], k, True).start()
        weight_copy(r, pair, share_w, k, True).start()

    @pl.when(jnp.logical_and(c == 0, c < last))
    def _():
        pl.semaphore_wait(go, len(row_peers) + jnp.where(r == 0, len(helpers), 0))
        tell((r, c + 1))

    def first_weights(k):
        filled(weights.at[pl.ds(0, len(near)), pl.ds(0, row_w)], recv_w.at[0, k])
        for dy, dx in diagonal:
            @pl.when(core == 0)
            def _():
                weight_copy(row_of(dy, 0), row_of(0, dx), recv_w.at[1, k], k).start()

            @pl.when(core == 1)
            def _():
                weight_copy(row_of(0, dx), row_of(dy, 0), recv_w.at[1, k], k).start()
        for source in near:
            weight_copy(source, pair, share_w, k).start()

    def far_weights(k):
        filled(weights.at[pl.ds(0, len(far)), pl.ds(0, row_w)], recv_w.at[1, k])
        for source in far:
            weight_copy(source, pair, share_w, k).start()

    source_at = functools.partial(nth_source, n_col, c)
    inner = jnp.logical_and(c > 0, c < last)

    def pass_acts(t, k):
        source = source_at(t)
        wait_acts(source, k)

        @pl.when(source < c)
        def _():
            act_copy(source, 1, k).start()

        @pl.when(source > c)
        def _():
            act_copy(source, 0, k).start()

    def help_out():
        for helper, k in helpers:
            @pl.when(jnp.logical_and(c == 1, r == helper))
            def _():
                filled(held, recv_h)
                held_copy(held, held, (r, 0), send_h, recv_h).start()

    def help_in():
        for helper, k in helpers:
            @pl.when(jnp.logical_and(c == 0, r == helper))
            def _():
                filled(held, recv_h)
                there = acts.at[1, pl.ds(starts_a[k], sizes_a[k])]
                held_copy(held, there, (0, 0), send_h, recv_a.at[0, k]).start()

    events = [(0.4 * tokens * width, "out", 0, 0), (1.1 * tokens * width, "in", 0, 0)]
    w_time, w_lag = row_w * hidden, tokens * width / 5
    for t in range(last):
        for k in range(n_a):
            events.append(((t // 2 * tokens + starts_a[k] + sizes_a[k]) * width, "a", t, k))
    for k in range(n_w):
        events.append(((k + 1) * w_time * (n_x + n_y - 2) / 2 + w_lag, "near", 0, k))
        events.append(((k + 2) * w_time * (n_x + n_y - 2) / 2 + w_time + w_lag, "far", 0, k))
    for _, kind, t, k in sorted(events):
        if kind == "a":
            pl.when(inner)(functools.partial(pass_acts, t, k))
        elif kind == "out":
            help_out()
        elif kind == "in":
            help_in()
        elif kind == "near":
            first_weights(k)
        elif diagonal:
            far_weights(k)
    filled(weights.at[pl.ds(0, n_row // 2 + 1)], share_w)
    own_a.wait()

    product = functools.partial(product_of, n_col, c, acts, weights)

    every = pl.ds(0, tokens)
    total[...] = product(c, every)

    @pl.loop(0, last - 1)
    def _(t):
        source = source_at(t)

        @pl.when(jnp.logical_not(inner))
        def _():
            for k in range(n_a):
                wait_acts(source, k)

        total[...] += product(source, every)

    final = source_at(last - 1)

    for k in range(n_a):
        rows = pl.ds(starts_a[k], sizes_a[k])

        pl.when(jnp.logical_not(inner))(functools.partial(wait_acts, final, k))

        if k == n_a - 1:
            break
        pre = total[rows, :] + product(final, rows)
        out[rows, :] = (pre / (1.0 + jnp.exp(-pre))).astype(out.dtype)

    for n in range(1, n_col):
        pl.when(jnp.logical_and(c < last, c + 1 == n))(functools.partial(filled, acts.at[pl.ds(0, n)], send_a.at[1]))
        pl.when(jnp.logical_and(c > 0, n_col - c == n))(functools.partial(filled, acts.at[pl.ds(0, n)], send_a.at[0]))
    for helper, _ in helpers:
        pl.when(jnp.logical_and(c < 2, r == helper))(functools.partial(filled, held, send_h))
    filled(weights.at[pl.ds(0, n_row - 1)], send_w)


def body(n_row, n_col, act_tiles, up_tiles):
    tokens, width = act_tiles.shape
    depth, hidden = up_tiles.shape
    chips = n_row // 2
    n_x = max(n for n in range(1, chips + 1) if chips % n == 0 and n * n <= chips)
    n_y = chips // n_x
    cuts, n_w = pieces_uneven(tokens, (6, 12, 2, 2, 2), 16), pieces_of(depth, 2, 16)
    n_a = len(cuts)
    held = pl.pallas_call(
        functools.partial(kernel, (n_y, n_x, n_col), (cuts, n_w)),
        out_shape=(
            pltpu.VMEM((tokens, hidden), jnp.bfloat16),
            pltpu.VMEM((n_col, tokens, width), jnp.bfloat16),
            pltpu.VMEM((n_row, depth, hidden), jnp.bfloat16),
            pltpu.VMEM((tokens, hidden), jnp.float32),
        ),
        in_specs=[pl.BlockSpec(memory_space=pltpu.HBM)] * 2,
        out_specs=(pl.BlockSpec(memory_space=pltpu.VMEM),) * 4,
        scratch_shapes=[
            pltpu.SemaphoreType.DMA((2,)),
            pltpu.SemaphoreType.DMA((max(n_col - 1, 1), n_a)),
            pltpu.SemaphoreType.DMA,
            pltpu.SemaphoreType.DMA((2, n_w)),
            pltpu.SemaphoreType.DMA,
            pltpu.SemaphoreType.DMA,
            pltpu.SemaphoreType.REGULAR,
            pltpu.VMEM((cuts[-1], width), jnp.bfloat16),
            pltpu.SemaphoreType.DMA,
            pltpu.SemaphoreType.DMA,
        ],
        compiler_params=pltpu.CompilerParams(collective_id=0, has_side_effects=True, vmem_limit_bytes=8000000),
        cost_estimate=pl.CostEstimate(
            flops=2 * tokens * width * n_col * hidden,
            bytes_accessed=2 * (act_tiles.size + up_tiles.size + tokens * hidden),
            transcendentals=tokens * hidden,
        ),
        name="gather_up_silu",
    )(*[pltpu.with_memory_space_constraint(a, pltpu.HBM) for a in (act_tiles, up_tiles)])
    return pl.pallas_call(
        functools.partial(finish, n_col, tokens - cuts[-1]),
        out_shape=jax.ShapeDtypeStruct((tokens, hidden), jnp.bfloat16),
        in_specs=[pl.BlockSpec(memory_space=pltpu.VMEM)] * 4,
        out_specs=pl.BlockSpec(memory_space=pltpu.HBM),
        scratch_shapes=[pltpu.VMEM((cuts[-1], hidden), jnp.bfloat16), pltpu.SemaphoreType.DMA((2,))],
        compiler_params=pltpu.CompilerParams(vmem_limit_bytes=8000000),
        name="last_rows",
    )(*[pltpu.with_memory_space_constraint(a, pltpu.VMEM) for a in held])


def solution(mesh):
    return jax.shard_map(
        functools.partial(body, mesh.shape["row"], mesh.shape["col"]),
        mesh=mesh,
        in_specs=(P("row", "col"), P("row", "col")),
        out_specs=P("row", "col"),
        check_vma=False,
    )
```
